32 devices in a mesh: seq: 16 (over z, x, core), head: 2 (over y).
Axes of the slice: x: 2, y: 2, z: 4, core: 2. Of those that a mesh axis runs over, the one named last changes fastest.
Arguments:
- queries: bfloat16 [8192, 8192], P('seq', 'head'), may hold values from -6 to 6
- key_rows: bfloat16 [8192, 8192], P('seq', 'head'), may hold values from -6 to 6
- values: bfloat16 [8192, 8192], P('seq', 'head'), may hold values from -360 to 360
- slopes: float32 [64], P('head'), may hold values from 3.6621094e-05 to 0.06, as said below
- doc_lengths: int32 [8], replicated, may hold values from 1 to 4096, 8192 in all
- norm_gain: float32 [8192], P('head'), may hold values from 0.1 to 1.9
Outputs:
- attended: bfloat16 [8192, 8192], P('seq', 'head')
The draws below stay inside these ranges and needn't reach their ends.
Inputs may be any that keep to these rules, and one draw needn't show every extreme that they name: `slopes`: each head's rate lies between 0.3 / 8192 and 0.06.
All inputs are finite; a program needn't handle non-finite values.
Results may differ from the reference program's by a relative error of at most 0.0056.
Values may be sent and summed in bfloat16 or wider, within the bound.
A program may use at most 128 MiB of HBM per device.

```python
import math
import jax
import jax.numpy as jnp
import numpy as np
from jax import lax

H = 64
DH = 128
BLOCK = 256
DOCS = 8
TOKENS = 8192
MOST = 4096


def draw_slopes(key, part):
    key_slow, key_fast, key_pick = jax.random.split(key, 3)
    lowest = math.log(0.3 / TOKENS)
    middle = math.log(2.3 / TOKENS)
    highest = math.log(0.06)
    slow_rates = jnp.exp(jax.random.uniform(key_slow, (H,), jnp.float32, lowest, middle))
    fast_rates = jnp.exp(jax.random.uniform(key_fast, (H,), jnp.float32, middle, highest))
    share = 0.5
    picked = jax.random.uniform(key_pick, (H,), jnp.float32) < share
    return jnp.where(picked, slow_rates, fast_rates).astype(jnp.float32)


def draw_values(key, part):
    key_main, key_cols = jax.random.split(key, 2)
    columns = jnp.arange(H * DH, dtype=jnp.int32)
    head_place = (columns // DH).astype(jnp.float32) / max(H - 1, 1)
    base_draw = jnp.clip(jax.random.normal(key_main, (TOKENS, H * DH), jnp.float32), -4.0, 4.0)
    head_ramp = jnp.exp(math.log(3.0) * head_place)
    column_scale = jnp.exp(jax.random.uniform(key_cols, (H * DH,), jnp.float32, 0.0, math.log(10.0)))
    return (base_draw * (head_ramp * column_scale)[None, :]).astype(jnp.bfloat16)


def block_levels(key, extent, pieces, least, high):
    factor_of = 1.0
    for axis_at, shards_of in pieces:
        draws = jax.random.uniform(jax.random.fold_in(jax.random.fold_in(key, 6), axis_at), (shards_of,), jnp.float32, least / len(pieces), high / len(pieces))
        factor_of = factor_of * jnp.repeat(jnp.exp(draws), extent[axis_at] // shards_of).reshape((-1,) + (1,) * (len(extent) - 1 - axis_at))
    return factor_of


def split_up(number_of, total, bound, lean):
    weights = [(1 << 20) // math.isqrt(grade ** lean) + 1 for grade in range(2, number_of + 1)]
    spare, holding = total - bound - (number_of - 1), [1] * (number_of - 1)
    while spare > 0:
        movable = [i for i in range(number_of - 1) if holding[i] < bound]
        mass, budget = sum([weights[i] for i in movable]), spare
        for i in movable:
            more = min(bound - holding[i], max(1, budget * weights[i] // mass), spare)
            holding[i] = holding[i] + more
            spare = spare - more
    return np.array([bound] + holding)


def uneven_parts(stream_key, amount, total, bound, skew):
    if amount == 2:
        one = jax.random.randint(stream_key, (), max(1, total - bound), min(bound, total - 1) + 1)
        return jnp.stack([one, total - one])
    sizes = jnp.asarray(split_up(amount, total, bound, skew), jnp.int32)
    pairs = (amount - 1) // 2
    source_of, receiver = sizes[1:1 + 2 * pairs:2], sizes[2:2 + 2 * pairs:2]
    room = jnp.minimum(source_of - 1, bound - receiver)
    passed = jax.random.randint(jax.random.fold_in(stream_key, 1), (pairs,), 0, 1 << 20) % (room + 1)
    sizes = sizes.at[1:1 + 2 * pairs:2].set(source_of - passed).at[2:2 + 2 * pairs:2].set(receiver + passed)
    return sizes[jax.random.permutation(jax.random.fold_in(stream_key, 2), amount)]


def noise(key, extent, width, most, cuts=(), held_as=jnp.bfloat16):
    level = block_levels(key, extent, cuts, -0.22, 0.18) if cuts else 1.0
    values = jax.random.normal(key, extent, jnp.float32) * width * level
    return jnp.minimum(jnp.maximum(values, -most), most).astype(held_as)


def setup_inputs(seed: int = 0) -> dict:
    key_of = jax.random.split(jax.random.key(seed), 7)
    queries = noise(key_of[0], (TOKENS, H * DH), 1.0, 6.0, ((0, 16), (1, 2)))
    key_rows = noise(key_of[1], (TOKENS, H * DH), 1.0, 6.0, ((0, 16), (1, 2)))
    values = draw_values(jax.random.fold_in(key_of[6], 71), 0)
    slopes = draw_slopes(jax.random.fold_in(key_of[6], 71), 0)
    doc_lengths = uneven_parts(key_of[4], DOCS, TOKENS, MOST, 2).astype(jnp.int32)
    norm_gain = jnp.clip(1.0 + 0.18 * jax.random.normal(key_of[5], (H * DH,), jnp.float32), 0.1, 1.9)
    return {"queries": queries, "key_rows": key_rows, "values": values, "slopes": slopes, "doc_lengths": doc_lengths, "norm_gain": norm_gain}


def segment_of(positions, doc_lengths):
    starts = jnp.cumsum(doc_lengths) - doc_lengths
    later_starts = starts[1:]
    counted = lax.optimization_barrier(jnp.sum((positions[..., None] >= later_starts).astype(jnp.int32), axis=-1))
    return jnp.where(positions < 0, -1, counted).astype(jnp.int32)

def reference(queries, key_rows, values, slopes, doc_lengths, norm_gain):
    blocks = TOKENS // BLOCK
    query_all = queries.reshape(blocks, BLOCK, H, DH)
    key_all = key_rows.reshape(blocks, BLOCK, H, DH)
    value_all = values.reshape(blocks, BLOCK, H, DH)
    offsets = jnp.arange(BLOCK, dtype=jnp.int32)
    lags = offsets[:, None] - offsets[None, :]

    def advance(state, inputs):
        query_block, key_block, value_block, index = inputs
        first = index * BLOCK
        positions = first + offsets
        segment = segment_of(positions, doc_lengths)
        before = segment_of(first - 1 + jnp.zeros((1,), jnp.int32), doc_lengths)[0]
        query_wide = query_block.astype(jnp.float32)
        key_wide = key_block.astype(jnp.float32)
        value_wide = value_block.astype(jnp.float32)
        allowed = (lags >= 0) & (segment[:, None] == segment[None, :])
        distance = jnp.maximum(lags, 0).astype(jnp.float32)
        decay_mask = jnp.where(allowed[None], jnp.exp(-slopes[:, None, None] * distance[None]), 0.0)
        scores = jnp.einsum('thd,shd->hts', query_wide, key_wide)
        weights = lax.optimization_barrier((scores * decay_mask).astype(jnp.bfloat16)).astype(jnp.float32)
        intra_part = jnp.einsum('hts,shd->thd', weights, value_wide)
        remaining = (BLOCK - 1 - offsets).astype(jnp.float32)
        scale_rows = jnp.where((segment == segment[-1])[:, None], jnp.exp(-slopes[None, :] * remaining[:, None]), 0.0)
        weighted = lax.optimization_barrier((scale_rows[:, :, None] * value_wide).astype(jnp.bfloat16)).astype(jnp.float32)
        local_state = jnp.einsum('shd,she->hde', key_wide, weighted)
        factor = jnp.where(before == segment[-1], jnp.exp(-slopes * BLOCK), 0.0)
        entering = lax.optimization_barrier(state.astype(jnp.bfloat16)).astype(jnp.float32)
        reach = (offsets + 1).astype(jnp.float32)
        carry_rows = jnp.where((segment == before)[:, None], jnp.exp(-slopes[None, :] * reach[:, None]), 0.0)
        inter_part = jnp.einsum('thd,hde->the', query_wide, entering) * carry_rows[:, :, None]
        mixed = (intra_part + inter_part).reshape(BLOCK, H * DH)
        mean_square = lax.optimization_barrier(jnp.mean(mixed * mixed, axis=1, keepdims=True))
        result = (mixed * lax.rsqrt(mean_square + 1e-05) * norm_gain[None, :]).astype(jnp.bfloat16)
        return (factor[:, None, None] * state + local_state, result)
    initial = jnp.zeros((H, DH, DH), jnp.float32)
    _, results = lax.scan(advance, initial, (query_all, key_all, value_all, jnp.arange(blocks, dtype=jnp.int32)))
    return results.reshape(TOKENS, H * DH)
```

```python
import functools

import jax
import jax.numpy as jnp
from jax import lax
from jax.experimental import pallas as pl
from jax.experimental.pallas import tpu as pltpu
from jax.sharding import PartitionSpec as P

BLOCK = 256
FAR = 1e30
LOG2E = 1.4426950408889634
F32 = jnp.float32
BF16 = jnp.bfloat16
MESH = pl.DeviceIdType.MESH
CUT = 1
HOP = 4
XLAG = 4
XTRIP = 4
CTRIP = 2
LATE = 2


def kernel(
    planes, head_parts, heads, blocks,
    slopes_hbm, docs_hbm, q_hbm, k_hbm, v_hbm,
    out_ref, inv_ref,
    q_ref, k_ref, v_ref, mixed_ref, local_ref, even_ref, odd_ref, own_ref, carry_ref, chip_ref,
    s_send, s_recv, c_send, c_recv, a_send, a_recv, p_send, p_recv, x_send, x_recv,
    lag_ref, same_ref, tail_ref, lead_ref, rem_ref, reach_ref, sq_ref, sq_send, sq_recv,
    slopes_ref, docs_ref, small_sem, k_sem, v_sem, q_sem,
    s_out, s_in, c_out, c_in, a_out, a_in, p_out, p_in, x_out, x_in, sq_out, sq_in,
):
    groups = heads // 4
    rows = blocks * BLOCK
    size = q_ref.shape[1] // heads
    piece = size // CUT
    late = min(LATE, groups)

    def load(hbm, ref, sem, w):
        wide = pl.ds(pl.multiple_of(w * 4 * size, 4 * size), 4 * size)
        return pltpu.make_async_copy(hbm.at[:, wide], ref.at[:, wide], sem.at[w])

    def each(count, body, start=0):
        def turn(i, _):
            body(i)
            return 0
        lax.fori_loop(start, count, turn, 0)

    def begin_kv(w):
        load(k_hbm, k_ref, k_sem, w).start()
        load(v_hbm, v_ref, v_sem, w).start()

    slopes_copy = pltpu.make_async_copy(slopes_hbm, slopes_ref, small_sem.at[0])
    docs_copy = pltpu.make_async_copy(docs_hbm, docs_ref, small_sem.at[1])
    begin_kv(0)
    docs_copy.start()
    slopes_copy.start()
    each(groups, begin_kv, 1)
    each(groups, lambda w: load(q_hbm, q_ref, q_sem, w).start())

    seq = lax.axis_index("seq")
    headpos = lax.axis_index("head")
    core = lax.rem(seq, 2)
    side = lax.rem(lax.div(seq, 2), 2)
    plane = lax.div(seq, 4)
    partner = seq + 1 - 2 * core
    across = seq + 2 - 4 * side
    ahead = jnp.minimum(seq + 4, 4 * planes - 1)

    barrier = pltpu.get_barrier_semaphore()
    pl.semaphore_signal(barrier, inc=1, device_id={"seq": partner}, device_id_type=MESH)
    pl.semaphore_signal(barrier, inc=1, device_id={"seq": across}, device_id_type=MESH)

    @pl.when(plane < planes - 1)
    def _():
        pl.semaphore_signal(barrier, inc=1, device_id={"seq": seq + 4}, device_id_type=MESH)

    @pl.when(plane > 0)
    def _():
        pl.semaphore_signal(barrier, inc=1, device_id={"seq": seq - 4}, device_id_type=MESH)

    for i in range(1, head_parts):
        pl.semaphore_signal(
            barrier, inc=1, device_id={"head": lax.rem(headpos + i, head_parts)}, device_id_type=MESH
        )

    def cols(h, wide=1):
        return pl.ds(pl.multiple_of(h * size, wide * size), wide * size)

    def remote(src, dst, first, count, sem_at, out_sem, in_sem, target):
        part = pl.ds(first, count)
        return pltpu.make_async_remote_copy(
            src_ref=src.at[part], dst_ref=dst.at[part],
            send_sem=out_sem.at[sem_at], recv_sem=in_sem.at[sem_at],
            device_id={"seq": target}, device_id_type=MESH,
        )

    def s_copy(w):
        return remote(s_send, s_recv, 2 * w * CUT, 2 * CUT, w, s_out, s_in, partner)

    def c_copy(n):
        return remote(c_send, c_recv, n, 1, n, c_out, c_in, partner)

    def a_copy(j):
        return remote(a_send, a_recv, j, 1, j, a_out, a_in, across)

    def p_copy(j):
        return remote(p_send, p_recv, j, 1, j, p_out, p_in, ahead)

    def x_copy(j):
        return remote(x_send, x_recv, j, 1, j, x_out, x_in, across)

    down = lax.broadcasted_iota(jnp.int32, (BLOCK, BLOCK), 0)
    along = lax.broadcasted_iota(jnp.int32, (BLOCK, BLOCK), 1)
    lag = jnp.where(down >= along, (down - along).astype(F32), F32(FAR))
    lag_ref[...] = lag[BLOCK // 2:]
    offs = lax.broadcasted_iota(jnp.int32, (BLOCK, size), 0)
    rem_ref[...] = (BLOCK - 1 - offs).astype(F32)
    reach_ref[...] = (offs + 1).astype(F32)
    sq_ref[...] = jnp.zeros_like(sq_ref)

    docs_copy.wait()
    slopes_copy.wait()
    starts = []
    total = jnp.int32(0)
    for j in range(docs_ref.shape[0] - 1):
        total = total + docs_ref[j]
        starts.append(total)

    def segment(pos):
        counted = jnp.zeros_like(pos)
        for s in starts:
            counted = counted + jnp.where(pos >= s, 1, 0)
        return jnp.where(pos < 0, -1, counted)

    def joined(a, b):
        return jnp.where(segment(a) == segment(b), F32(1), F32(0))

    base = seq * rows
    chip = base - core * rows
    within = []
    for b in range(blocks):
        b0 = base + b * BLOCK
        row_seg = segment(b0 + offs)
        tail_ref[b] = jnp.where(row_seg == segment(b0 + BLOCK - 1), F32(1), F32(0))
        lead_ref[b] = jnp.where(row_seg == segment(b0 - 1), F32(1), F32(0))
        within.append(joined(b0 - 1, b0 + BLOCK - 1))
    board = chip - 2 * side * rows
    j_cores = joined(chip + rows - 1, chip + 2 * rows - 1)
    j_enter = joined(chip - 1, chip + rows - 1)
    j_chips = joined(board + 2 * rows - 1, board + 4 * rows - 1)
    j_board = joined(board - 1, board + 4 * rows - 1)
    j_front = joined(board - 1, board + 2 * rows - 1)

    def rate(h):
        return slopes_ref[h] * F32(-LOG2E)

    def fade(h, distance, keep):
        return jnp.exp2(jnp.full((1, size), rate(h) * distance, F32)) * keep

    @pl.when(plane == 0)
    def _():
        p_recv[...] = jnp.zeros_like(p_recv)

    def end_state(h):
        scale = jnp.exp2(rem_ref[...] * rate(h))
        state = None
        for b in range(blocks):
            here = pl.ds(b * BLOCK, BLOCK)
            weighted = (scale * tail_ref[b] * v_ref[here, cols(h)].astype(F32)).astype(BF16)
            one = lax.dot_general(
                k_ref[here, cols(h)], weighted, (((0,), (0,)), ((), ())), preferred_element_type=F32
            )
            if b < blocks - 1:
                local_ref[b, h] = one
            state = one if state is None else fade(h, F32(BLOCK), within[b]) * state + one
        return state

    def cut(i):
        return slice(i * piece, (i + 1) * piece)

    def ends(w):
        load(k_hbm, k_ref, k_sem, w).wait()
        load(v_hbm, v_ref, v_sem, w).wait()
        for b0 in range(2):
            state = end_state(4 * w + 2 * (1 - core) + b0).astype(BF16)
            for i in range(CUT):
                s_send[(2 * w + b0) * CUT + i] = state[cut(i)]
        for b0 in range(2):
            state = end_state(4 * w + 2 * core + b0)
            for i in range(CUT):
                own_ref[(2 * w + b0) * CUT + i] = state[cut(i)]

    is_second = core == 1
    is_after = side == 1

    def core_states(n):
        here, there = own_ref[n], s_recv[n].astype(F32)
        return jnp.where(is_second, there, here), jnp.where(is_second, here, there)

    def chip_state(h, n):
        early, late_one = core_states(n)
        return fade(h, F32(rows), j_cores) * early + late_one

    def give_head(w):
        return 4 * w + 2 * core + (1 - side)

    def keep_head(w):
        return 4 * w + 2 * core + side

    def give(w):
        s_copy(w).wait_recv()
        for i in range(CUT):
            n = (2 * w + (1 - side)) * CUT + i
            a_send[w * CUT + i] = chip_state(give_head(w), n).astype(BF16)
        for i in range(CUT):
            a_copy(w * CUT + i).start()
        for i in range(CUT):
            n = (2 * w + side) * CUT + i
            chip_ref[w * CUT + i] = chip_state(keep_head(w), n)

    def settle(h, n, enters):
        early, _ = core_states(n)
        second = fade(h, F32(rows), j_enter) * enters + early
        carry_ref[n] = jnp.where(is_second, second, enters)
        c_send[n] = jnp.where(is_second, enters, second).astype(BF16)
        c_copy(n).start()

    def chain(w):
        h = keep_head(w)
        for i in range(CUT):
            j = w * CUT + i
            a_copy(j).wait_recv()

            @pl.when(plane > 0)
            def _():
                p_copy(j).wait_recv()

            here, there = chip_ref[j], a_recv[j].astype(F32)
            early, late_one = jnp.where(is_after, there, here), jnp.where(is_after, here, there)
            before = p_recv[j].astype(F32)
            total = fade(h, F32(2 * rows), j_chips) * early + late_one
            p_send[j] = (fade(h, F32(4 * rows), j_board) * before + total).astype(BF16)

            @pl.when(plane < planes - 1)
            def _():
                p_copy(j).start()

            second = fade(h, F32(2 * rows), j_front) * before + early
            x_send[j] = jnp.where(is_after, before, second).astype(BF16)

            @pl.when(plane * HOP >= XLAG)
            def _():
                x_copy(j).start()

            settle(h, (2 * w + side) * CUT + i, jnp.where(is_after, second, before))

    def x_start(w):
        for i in range(CUT):
            x_copy(w * CUT + i).start()

    def over(w):
        for i in range(CUT):
            j = w * CUT + i
            x_copy(j).wait_recv()
            settle(give_head(w), (2 * w + (1 - side)) * CUT + i, x_recv[j].astype(F32))

    mid = BLOCK // 2
    for ref in (even_ref, odd_ref):
        for i in range(2):
            for b in range(blocks):
                ref[i, b, :mid, mid:] = jnp.zeros((mid, BLOCK - mid), BF16)

    for b in range(blocks):
        b0 = base + b * BLOCK
        same_ref[b] = jnp.where(segment(b0 + down) == segment(b0 + along), F32(1), F32(0))

    def weigh(u, ref):
        for i in range(2):
            h = 2 * u + i
            decay = jnp.exp2(lag_ref[...] * rate(h))
            for b in range(blocks):
                here = pl.ds(b * BLOCK, BLOCK)
                scores = lax.dot_general(
                    q_ref[here, cols(h)], k_ref[here, cols(h)], (((1,), (1,)), ((), ())),
                    preferred_element_type=F32,
                )
                ref[i, b, :mid, :mid] = (
                    scores[:mid, :mid] * decay[:, mid:] * same_ref[b, :mid, :mid]
                ).astype(BF16)
                ref[i, b, mid:, :] = (scores[mid:] * decay * same_ref[b, mid:, :]).astype(BF16)

    def apply(u, ref):
        for i in range(2):
            h = 2 * u + i
            for b in range(blocks):
                here = pl.ds(b * BLOCK, BLOCK)
                mixed_ref[here, cols(h)] = jnp.dot(
                    ref[i, b], v_ref[here, cols(h)], preferred_element_type=F32
                )

    units = heads // 2

    def intra(u):
        following = jnp.minimum(u + 1, units - 1)

        @pl.when(lax.rem(u, 2) == 0)
        def _():
            weigh(following, odd_ref)
            apply(u, even_ref)

        @pl.when((lax.rem(u, 2) == 1) & (u < units - 1))
        def _():
            load(q_hbm, q_ref, q_sem, lax.div(following, 2)).wait()

        @pl.when(lax.rem(u, 2) == 1)
        def _():
            weigh(following, even_ref)
            apply(u, odd_ref)

    def finish(h, states):
        blank = jnp.zeros((size, size), BF16)
        for b in range(blocks):
            first, second = states[0].astype(BF16), states[1].astype(BF16)
            joint = jnp.concatenate(
                [jnp.concatenate([first, blank], axis=1), jnp.concatenate([blank, second], axis=1)],
                axis=0,
            )
            for r in range(0, BLOCK, BLOCK // 2):
                here = pl.ds(b * BLOCK + r, BLOCK // 2)
                inter = jnp.dot(q_ref[here, cols(h, 2)], joint, preferred_element_type=F32)
                squares = sq_ref[here, :]
                reach = reach_ref[r:r + BLOCK // 2]
                lead = lead_ref[b, r:r + BLOCK // 2]
                for i in range(2):
                    scale = jnp.exp2(reach * rate(h + i)) * lead
                    mixed = mixed_ref[here, cols(h + i)] + inter[:, i * size:(i + 1) * size] * scale
                    squares = squares + mixed * mixed
                    out_ref[here, cols(h + i)] = mixed.astype(BF16)
                sq_ref[here, :] = squares
            if b < blocks - 1:
                states = [
                    fade(h + i, F32(BLOCK), within[b]) * states[i] + local_ref[b, h + i]
                    for i in range(2)
                ]

    def whole(ref, w, b0):
        parts = [ref[(2 * w + b0) * CUT + i] for i in range(CUT)]
        return parts[0] if CUT == 1 else jnp.concatenate(parts, axis=0)

    def mine(w):
        finish(4 * w + 2 * core, [whole(carry_ref, w, b0) for b0 in range(2)])

    def theirs(w):
        for i in range(2 * CUT):
            c_copy(2 * w * CUT + i).wait_recv()
        finish(4 * w + 2 * (1 - core), [whole(c_recv, w, b0).astype(F32) for b0 in range(2)])

    def ends_step(w):
        ends(w)

        @pl.when(w == 0)
        def _():
            beside = jnp.where(plane > 0, 1, 0) + jnp.where(plane < planes - 1, 1, 0)
            pl.semaphore_wait(barrier, 1 + head_parts + beside)

        s_copy(w).start()

        @pl.when(w >= late)
        def _():
            give(w - late)

    each(groups, ends_step)
    load(q_hbm, q_ref, q_sem, 0).wait()
    weigh(jnp.int32(0), even_ref)

    chain_at = HOP * plane
    x_at = jnp.maximum(chain_at, XLAG)
    over_at = x_at + XTRIP
    mine_at = jnp.maximum(over_at, units)
    last_over = max(HOP * (planes - 1), XLAG) + XTRIP
    slots = max(last_over, units) + groups + CTRIP

    def when_in(t, start, count, body):
        @pl.when((t >= start) & (t < start + count))
        def _():
            body(t - start)

    def slot(t):
        when_in(t, 0, late, lambda n: give(groups - late + n))
        when_in(t, chain_at, groups, chain)

        @pl.when(chain_at < XLAG)
        def _():
            when_in(t, x_at, groups, x_start)

        when_in(t, over_at, groups, over)
        when_in(t, 0, units, intra)
        when_in(t, mine_at, groups, mine)
        when_in(t, mine_at + CTRIP, groups, theirs)

    each(slots, slot)

    ones = jnp.ones((8, size), F32)
    summed = lax.dot_general(
        ones, sq_ref[...], (((1,), (1,)), ((), ())),
        precision=lax.Precision.HIGHEST, preferred_element_type=F32,
    )
    sq_send[...] = summed

    def sq_copy(i):
        return pltpu.make_async_remote_copy(
            src_ref=sq_send, dst_ref=sq_recv.at[i], send_sem=sq_out.at[i], recv_sem=sq_in.at[i],
            device_id={"head": lax.rem(headpos + i, head_parts)}, device_id_type=MESH,
        )

    for i in range(1, head_parts):
        sq_copy(i).start()

    each(groups, lambda w: s_copy(w).wait_send())
    each(2 * groups * CUT, lambda n: c_copy(n).wait_send())

    def drain(j):
        a_copy(j).wait_send()
        x_copy(j).wait_send()

        @pl.when(plane < planes - 1)
        def _():
            p_copy(j).wait_send()

    each(groups * CUT, drain)
    for i in range(1, head_parts):
        sq_copy(i).wait_recv()
        summed = summed + sq_recv[i]
    inverse = lax.rsqrt(summed / F32(heads * size * head_parts) + F32(1e-05))
    inv_ref[...] = jnp.broadcast_to(jnp.transpose(inverse)[:, 0:1], inv_ref.shape)
    for i in range(1, head_parts):
        sq_copy(i).wait_send()


def scale_kernel(mixed_ref, inv_ref, gain_ref, final_hbm, final_ref, sem):
    rows, size = inv_ref.shape
    strip = rows // sem.shape[0]

    def move(i):
        here = pl.ds(i * strip, strip)
        return pltpu.make_async_copy(final_ref.at[here], final_hbm.at[here], sem.at[i])

    for i in range(sem.shape[0]):
        here = pl.ds(i * strip, strip)
        inverse = inv_ref[here, :]
        for c in range(0, final_ref.shape[1], size):
            piece = mixed_ref[here, c:c + size].astype(F32)
            final_ref[here, c:c + size] = (piece * inverse * gain_ref[:, c:c + size]).astype(BF16)
        move(i).start()
    for i in range(sem.shape[0]):
        move(i).wait()


def shards(planes, head_parts, queries, key_rows, values, slopes, doc_lengths, norm_gain):
    rows, feat = queries.shape
    heads = slopes.shape[0]
    size = feat // heads
    blocks = rows // BLOCK
    groups = heads // 4
    hbm = pl.BlockSpec(memory_space=pltpu.HBM)
    piece = size // CUT
    states = lambda count, dtype: pltpu.VMEM((count * CUT, piece, size), dtype)
    dma = lambda n: pltpu.SemaphoreType.DMA((n,))
    mixed, inverse = pl.pallas_call(
        functools.partial(kernel, planes, head_parts, heads, blocks),
        out_shape=(
            jax.ShapeDtypeStruct((rows, feat), BF16),
            jax.ShapeDtypeStruct((rows, size), F32),
        ),
        in_specs=[hbm] * 5,
        out_specs=(pl.BlockSpec(memory_space=pltpu.VMEM), pl.BlockSpec(memory_space=pltpu.VMEM)),
        scratch_shapes=[
            pltpu.VMEM((rows, feat), BF16),
            pltpu.VMEM((rows, feat), BF16),
            pltpu.VMEM((rows, feat), BF16),
            pltpu.VMEM((rows, feat), F32),
            pltpu.VMEM((max(blocks - 1, 1), heads, size, size), F32),
            pltpu.VMEM((2, blocks, BLOCK, BLOCK), BF16),
            pltpu.VMEM((2, blocks, BLOCK, BLOCK), BF16),
            states(2 * groups, F32),
            states(2 * groups, F32),
            states(groups, F32),
            *[states(2 * groups, BF16)] * 4,
            *[states(groups, BF16)] * 6,
            pltpu.VMEM((BLOCK // 2, BLOCK), F32),
            pltpu.VMEM((blocks, BLOCK, BLOCK), F32),
            pltpu.VMEM((blocks, BLOCK, size), F32),
            pltpu.VMEM((blocks, BLOCK, size), F32),
            pltpu.VMEM((BLOCK, size), F32),
            pltpu.VMEM((BLOCK, size), F32),
            pltpu.VMEM((rows, size), F32),
            pltpu.VMEM((8, rows), F32),
            pltpu.VMEM((head_parts, 8, rows), F32),
            pltpu.SMEM(slopes.shape, F32),
            pltpu.SMEM(doc_lengths.shape, jnp.int32),
            dma(2),
            *[dma(groups)] * 3,
            *[dma(groups)] * 2,
            *[dma(2 * groups * CUT)] * 2,
            *[dma(groups * CUT)] * 6,
            dma(head_parts),
            dma(head_parts),
        ],
        compiler_params=pltpu.CompilerParams(
            collective_id=0, has_side_effects=True, vmem_limit_bytes=47 * 1024 * 1024
        ),
    )(slopes, doc_lengths, queries, key_rows, values)
    vmem = pl.BlockSpec(memory_space=pltpu.VMEM)
    return pl.pallas_call(
        scale_kernel,
        out_shape=jax.ShapeDtypeStruct((rows, feat), BF16),
        in_specs=[vmem, vmem, vmem],
        out_specs=pl.BlockSpec(memory_space=pltpu.HBM),
        scratch_shapes=[pltpu.VMEM((rows, feat), BF16), pltpu.SemaphoreType.DMA((8,))],
        compiler_params=pltpu.CompilerParams(vmem_limit_bytes=9 * 1024 * 1024),
    )(mixed, inverse, norm_gain.reshape(1, feat))


def solution(mesh):
    placed = (P("seq", "head"), P("seq", "head"), P("seq", "head"), P("head"), P(), P("head"))
    return jax.shard_map(
        functools.partial(shards, mesh.shape["seq"] // 4, mesh.shape["head"]),
        mesh=mesh, in_specs=placed, out_specs=P("seq", "head"), check_vma=False,
    )
```

```python
import functools

import jax
import jax.numpy as jnp
from jax import lax
from jax.experimental import pallas as pl
from jax.experimental.pallas import tpu as pltpu
from jax.sharding import PartitionSpec as P

BLOCK = 256
FAR = 1e30
LOG2E = 1.4426950408889634
F32 = jnp.float32
BF16 = jnp.bfloat16
MESH = pl.DeviceIdType.MESH
CUT = 1
HOP = 4
XLAG = 4
XTRIP = 4
CTRIP = 2
LATE = 2


def kernel(
    planes, head_parts, heads, blocks,
    slopes_hbm, docs_hbm, q_hbm, k_hbm, v_hbm,
    out_ref, inv_ref,
    q_ref, k_ref, v_ref, mixed_ref, local_ref, even_ref, odd_ref, own_ref, carry_ref, chip_ref,
    s_send, s_recv, c_send, c_recv, a_send, a_recv, p_send, p_recv, x_send, x_recv,
    lag_ref, same_ref, tail_ref, lead_ref, sq_ref, sq_send, sq_recv,
    slopes_ref, docs_ref, small_sem, k_sem, v_sem, q_sem,
    s_out, s_in, c_out, c_in, a_out, a_in, p_out, p_in, x_out, x_in, sq_out, sq_in,
):
    groups = heads // 4
    rows = blocks * BLOCK
    size = q_ref.shape[1] // heads
    piece = size // CUT
    late = min(LATE, groups)

    def load(hbm, ref, sem, w):
        wide = pl.ds(pl.multiple_of(w * 4 * size, 4 * size), 4 * size)
        return pltpu.make_async_copy(hbm.at[:, wide], ref.at[:, wide], sem.at[w])

    def each(count, body, start=0):
        def turn(i, _):
            body(i)
            return 0
        lax.fori_loop(start, count, turn, 0)

    def begin_kv(w):
        load(k_hbm, k_ref, k_sem, w).start()
        load(v_hbm, v_ref, v_sem, w).start()

    slopes_copy = pltpu.make_async_copy(slopes_hbm, slopes_ref, small_sem.at[0])
    docs_copy = pltpu.make_async_copy(docs_hbm, docs_ref, small_sem.at[1])
    begin_kv(0)
    docs_copy.start()
    slopes_copy.start()
    each(groups, begin_kv, 1)
    each(groups, lambda w: load(q_hbm, q_ref, q_sem, w).start())

    seq = lax.axis_index("seq")
    headpos = lax.axis_index("head")
    core = lax.rem(seq, 2)
    side = lax.rem(lax.div(seq, 2), 2)
    plane = lax.div(seq, 4)
    partner = seq + 1 - 2 * core
    across = seq + 2 - 4 * side
    ahead = jnp.minimum(seq + 4, 4 * planes - 1)

    barrier = pltpu.get_barrier_semaphore()
    pl.semaphore_signal(barrier, inc=1, device_id={"seq": partner}, device_id_type=MESH)
    pl.semaphore_signal(barrier, inc=1, device_id={"seq": across}, device_id_type=MESH)

    @pl.when(plane < planes - 1)
    def _():
        pl.semaphore_signal(barrier, inc=1, device_id={"seq": seq + 4}, device_id_type=MESH)

    @pl.when(plane > 0)
    def _():
        pl.semaphore_signal(barrier, inc=1, device_id={"seq": seq - 4}, device_id_type=MESH)

    for i in range(1, head_parts):
        pl.semaphore_signal(
            barrier, inc=1, device_id={"head": lax.rem(headpos + i, head_parts)}, device_id_type=MESH
        )

    def cols(h, wide=1):
        return pl.ds(pl.multiple_of(h * size, wide * size), wide * size)

    def remote(src, dst, first, count, sem_at, out_sem, in_sem, target):
        part = pl.ds(first, count)
        return pltpu.make_async_remote_copy(
            src_ref=src.at[part], dst_ref=dst.at[part],
            send_sem=out_sem.at[sem_at], recv_sem=in_sem.at[sem_at],
            device_id={"seq": target}, device_id_type=MESH,
        )

    def s_copy(w):
        return remote(s_send, s_recv, 2 * w * CUT, 2 * CUT, w, s_out, s_in, partner)

    def c_copy(n):
        return remote(c_send, c_recv, n, 1, n, c_out, c_in, partner)

    def a_copy(j):
        return remote(a_send, a_recv, j, 1, j, a_out, a_in, across)

    def p_copy(j):
        return remote(p_send, p_recv, j, 1, j, p_out, p_in, ahead)

    def x_copy(j):
        return remote(x_send, x_recv, j, 1, j, x_out, x_in, across)

    down = lax.broadcasted_iota(jnp.int32, (BLOCK, BLOCK), 0)
    along = lax.broadcasted_iota(jnp.int32, (BLOCK, BLOCK), 1)
    lag = jnp.where(down >= along, (down - along).astype(F32), F32(FAR))
    lag_ref[...] = lag[BLOCK // 2:]
    offs = lax.broadcasted_iota(jnp.int32, (BLOCK, size), 0)
    rem = (BLOCK - 1 - offs).astype(F32)
    reach = (offs + 1).astype(F32)
    sq_ref[...] = jnp.zeros_like(sq_ref)

    docs_copy.wait()
    slopes_copy.wait()
    starts = []
    total = jnp.int32(0)
    for j in range(docs_ref.shape[0] - 1):
        total = total + docs_ref[j]
        starts.append(total)

    def segment(pos):
        counted = jnp.zeros_like(pos)
        for s in starts:
            counted = counted + jnp.where(pos >= s, 1, 0)
        return jnp.where(pos < 0, -1, counted)

    def joined(a, b):
        return jnp.where(segment(a) == segment(b), F32(1), F32(0))

    base = seq * rows
    chip = base - core * rows
    within = []
    for b in range(blocks):
        b0 = base + b * BLOCK
        row_seg = segment(b0 + offs)
        tail_ref[b] = jnp.where(row_seg == segment(b0 + BLOCK - 1), rem, F32(FAR))
        lead_ref[b] = jnp.where(row_seg == segment(b0 - 1), reach, F32(FAR))
        within.append(joined(b0 - 1, b0 + BLOCK - 1))
    board = chip - 2 * side * rows
    j_cores = joined(chip + rows - 1, chip + 2 * rows - 1)
    j_enter = joined(chip - 1, chip + rows - 1)
    j_chips = joined(board + 2 * rows - 1, board + 4 * rows - 1)
    j_board = joined(board - 1, board + 4 * rows - 1)
    j_front = joined(board - 1, board + 2 * rows - 1)

    def rate(h):
        return slopes_ref[h] * F32(-LOG2E)

    def fade(h, distance, keep):
        return jnp.exp2(jnp.full((1, size), rate(h) * distance, F32)) * keep

    @pl.when(plane == 0)
    def _():
        p_recv[...] = jnp.zeros_like(p_recv)

    def end_state(h):
        state = None
        for b in range(blocks):
            here = pl.ds(b * BLOCK, BLOCK)
            scale = jnp.exp2(tail_ref[b] * rate(h))
            weighted = (scale * v_ref[here, cols(h)].astype(F32)).astype(BF16)
            one = lax.dot_general(
                k_ref[here, cols(h)], weighted, (((0,), (0,)), ((), ())), preferred_element_type=F32
            )
            if b < blocks - 1:
                local_ref[b, h] = one
            state = one if state is None else fade(h, F32(BLOCK), within[b]) * state + one
        return state

    def cut(i):
        return slice(i * piece, (i + 1) * piece)

    def ends(w):
        load(k_hbm, k_ref, k_sem, w).wait()
        load(v_hbm, v_ref, v_sem, w).wait()
        for b0 in range(2):
            state = end_state(4 * w + 2 * (1 - core) + b0).astype(BF16)
            for i in range(CUT):
                s_send[(2 * w + b0) * CUT + i] = state[cut(i)]
        for b0 in range(2):
            state = end_state(4 * w + 2 * core + b0)
            for i in range(CUT):
                own_ref[(2 * w + b0) * CUT + i] = state[cut(i)]

    is_second = core == 1
    is_after = side == 1

    def core_states(n):
        here, there = own_ref[n], s_recv[n].astype(F32)
        return jnp.where(is_second, there, here), jnp.where(is_second, here, there)

    def chip_state(h, n):
        early, late_one = core_states(n)
        return fade(h, F32(rows), j_cores) * early + late_one

    def give_head(w):
        return 4 * w + 2 * core + (1 - side)

    def keep_head(w):
        return 4 * w + 2 * core + side

    def give(w):
        s_copy(w).wait_recv()
        for i in range(CUT):
            n = (2 * w + (1 - side)) * CUT + i
            a_send[w * CUT + i] = chip_state(give_head(w), n).astype(BF16)
        for i in range(CUT):
            a_copy(w * CUT + i).start()
        for i in range(CUT):
            n = (2 * w + side) * CUT + i
            chip_ref[w * CUT + i] = chip_state(keep_head(w), n)

    def settle(h, n, enters):
        early, _ = core_states(n)
        second = fade(h, F32(rows), j_enter) * enters + early
        carry_ref[n] = jnp.where(is_second, second, enters)
        c_send[n] = jnp.where(is_second, enters, second).astype(BF16)
        c_copy(n).start()

    def chain(w):
        h = keep_head(w)
        for i in range(CUT):
            j = w * CUT + i
            a_copy(j).wait_recv()

            @pl.when(plane > 0)
            def _():
                p_copy(j).wait_recv()

            here, there = chip_ref[j], a_recv[j].astype(F32)
            early, late_one = jnp.where(is_after, there, here), jnp.where(is_after, here, there)
            before = p_recv[j].astype(F32)
            total = fade(h, F32(2 * rows), j_chips) * early + late_one
            p_send[j] = (fade(h, F32(4 * rows), j_board) * before + total).astype(BF16)

            @pl.when(plane < planes - 1)
            def _():
                p_copy(j).start()

            second = fade(h, F32(2 * rows), j_front) * before + early
            x_send[j] = jnp.where(is_after, before, second).astype(BF16)

            @pl.when(plane * HOP >= XLAG)
            def _():
                x_copy(j).start()

            settle(h, (2 * w + side) * CUT + i, jnp.where(is_after, second, before))

    def x_start(w):
        for i in range(CUT):
            x_copy(w * CUT + i).start()

    def over(w):
        for i in range(CUT):
            j = w * CUT + i
            x_copy(j).wait_recv()
            settle(give_head(w), (2 * w + (1 - side)) * CUT + i, x_recv[j].astype(F32))

    mid = BLOCK // 2
    for ref in (even_ref, odd_ref):
        for i in range(2):
            for b in range(blocks):
                ref[i, b, :mid, mid:] = jnp.zeros((mid, BLOCK - mid), BF16)

    for b in range(blocks):
        b0 = base + b * BLOCK
        same_ref[b] = jnp.where(segment(b0 + down) == segment(b0 + along), F32(1), F32(0))

    def weigh_one(u, ref, i, b, decay):
        h = 2 * u + i
        here = pl.ds(b * BLOCK, BLOCK)
        scores = lax.dot_general(
            q_ref[here, cols(h)], k_ref[here, cols(h)], (((1,), (1,)), ((), ())),
            preferred_element_type=F32,
        )
        ref[i, b, :mid, :mid] = (
            scores[:mid, :mid] * decay[:, mid:] * same_ref[b, :mid, :mid]
        ).astype(BF16)
        ref[i, b, mid:, :] = (scores[mid:] * decay * same_ref[b, mid:, :]).astype(BF16)

    def apply_one(u, ref, i, b):
        h = 2 * u + i
        here = pl.ds(b * BLOCK, BLOCK)
        mixed_ref[here, cols(h)] = jnp.dot(
            ref[i, b], v_ref[here, cols(h)], preferred_element_type=F32
        )

    def weigh(u, ref):
        for i in range(2):
            decay = jnp.exp2(lag_ref[...] * rate(2 * u + i))
            for b in range(blocks):
                weigh_one(u, ref, i, b, decay)

    def apply(u, ref):
        for i in range(2):
            for b in range(blocks):
                apply_one(u, ref, i, b)

    units = heads // 2

    def both(f, fref, u, uref):
        apply(u, uref)
        weigh(f, fref)

    def intra(u):
        following = jnp.minimum(u + 1, units - 1)

        @pl.when(lax.rem(u, 2) == 0)
        def _():
            both(following, odd_ref, u, even_ref)

        @pl.when((lax.rem(u, 2) == 1) & (u < units - 1))
        def _():
            load(q_hbm, q_ref, q_sem, lax.div(following, 2)).wait()

        @pl.when(lax.rem(u, 2) == 1)
        def _():
            both(following, even_ref, u, odd_ref)

    def finish(h, states):
        blank = jnp.zeros((size, size), BF16)
        for b in range(blocks):
            first, second = states[0].astype(BF16), states[1].astype(BF16)
            joint = jnp.concatenate(
                [jnp.concatenate([first, blank], axis=1), jnp.concatenate([blank, second], axis=1)],
                axis=0,
            )
            for r in range(0, BLOCK, BLOCK // 2):
                here = pl.ds(b * BLOCK + r, BLOCK // 2)
                inter = jnp.dot(q_ref[here, cols(h, 2)], joint, preferred_element_type=F32)
                squares = sq_ref[here, :]
                lead = lead_ref[b, r:r + BLOCK // 2]
                for i in range(2):
                    scale = jnp.exp2(lead * rate(h + i))
                    mixed = mixed_ref[here, cols(h + i)] + inter[:, i * size:(i + 1) * size] * scale
                    squares = squares + mixed * mixed
                    out_ref[here, cols(h + i)] = mixed.astype(BF16)
                sq_ref[here, :] = squares
            if b < blocks - 1:
                states = [
                    fade(h + i, F32(BLOCK), within[b]) * states[i] + local_ref[b, h + i]
                    for i in range(2)
                ]

    def whole(ref, w, b0):
        parts = [ref[(2 * w + b0) * CUT + i] for i in range(CUT)]
        return parts[0] if CUT == 1 else jnp.concatenate(parts, axis=0)

    def mine(w):
        finish(4 * w + 2 * core, [whole(carry_ref, w, b0) for b0 in range(2)])

    def theirs(w):
        for i in range(2 * CUT):
            c_copy(2 * w * CUT + i).wait_recv()
        finish(4 * w + 2 * (1 - core), [whole(c_recv, w, b0).astype(F32) for b0 in range(2)])

    def ends_step(w):
        ends(w)

        @pl.when(w == 0)
        def _():
            beside = jnp.where(plane > 0, 1, 0) + jnp.where(plane < planes - 1, 1, 0)
            pl.semaphore_wait(barrier, 1 + head_parts + beside)

        s_copy(w).start()

        @pl.when(w >= late)
        def _():
            give(w - late)

    each(groups, ends_step)
    load(q_hbm, q_ref, q_sem, 0).wait()
    weigh(jnp.int32(0), even_ref)

    chain_at = HOP * plane
    x_at = jnp.maximum(chain_at, XLAG)
    over_at = x_at + XTRIP
    mine_at = jnp.maximum(over_at, units)
    last_over = max(HOP * (planes - 1), XLAG) + XTRIP
    slots = max(last_over, units) + groups + CTRIP

    def when_in(t, start, count, body):
        @pl.when((t >= start) & (t < start + count))
        def _():
            body(t - start)

    def slot(t):
        when_in(t, 0, late, lambda n: give(groups - late + n))
        when_in(t, chain_at, groups, chain)

        @pl.when(chain_at < XLAG)
        def _():
            when_in(t, x_at, groups, x_start)

        when_in(t, over_at, groups, over)
        when_in(t, 0, units, intra)
        when_in(t, mine_at, groups, mine)
        when_in(t, mine_at + CTRIP, groups, theirs)

    each(slots, slot)

    ones = jnp.ones((8, size), F32)
    summed = lax.dot_general(
        ones, sq_ref[...], (((1,), (1,)), ((), ())),
        precision=lax.Precision.HIGHEST, preferred_element_type=F32,
    )
    sq_send[...] = summed

    def sq_copy(i):
        return pltpu.make_async_remote_copy(
            src_ref=sq_send, dst_ref=sq_recv.at[i], send_sem=sq_out.at[i], recv_sem=sq_in.at[i],
            device_id={"head": lax.rem(headpos + i, head_parts)}, device_id_type=MESH,
        )

    for i in range(1, head_parts):
        sq_copy(i).start()

    each(groups, lambda w: s_copy(w).wait_send())
    each(2 * groups * CUT, lambda n: c_copy(n).wait_send())

    def drain(j):
        a_copy(j).wait_send()
        x_copy(j).wait_send()

        @pl.when(plane < planes - 1)
        def _():
            p_copy(j).wait_send()

    each(groups * CUT, drain)
    for i in range(1, head_parts):
        sq_copy(i).wait_recv()
        summed = summed + sq_recv[i]
    inverse = lax.rsqrt(summed / F32(heads * size * head_parts) + F32(1e-05))
    inv_ref[...] = jnp.broadcast_to(jnp.transpose(inverse)[:, 0:1], inv_ref.shape)
    for i in range(1, head_parts):
        sq_copy(i).wait_send()


def scale_kernel(mixed_ref, inv_ref, gain_ref, final_hbm, final_ref, sem):
    rows, size = inv_ref.shape
    strip = rows // sem.shape[0]

    def move(i):
        here = pl.ds(i * strip, strip)
        return pltpu.make_async_copy(final_ref.at[here], final_hbm.at[here], sem.at[i])

    for i in range(sem.shape[0]):
        here = pl.ds(i * strip, strip)
        inverse = inv_ref[here, :]
        for c in range(0, final_ref.shape[1], size):
            piece = mixed_ref[here, c:c + size].astype(F32)
            final_ref[here, c:c + size] = (piece * inverse * gain_ref[:, c:c + size]).astype(BF16)
        move(i).start()
    for i in range(sem.shape[0]):
        move(i).wait()


def shards(planes, head_parts, queries, key_rows, values, slopes, doc_lengths, norm_gain):
    rows, feat = queries.shape
    heads = slopes.shape[0]
    size = feat // heads
    blocks = rows // BLOCK
    groups = heads // 4
    hbm = pl.BlockSpec(memory_space=pltpu.HBM)
    piece = size // CUT
    states = lambda count, dtype: pltpu.VMEM((count * CUT, piece, size), dtype)
    dma = lambda n: pltpu.SemaphoreType.DMA((n,))
    mixed, inverse = pl.pallas_call(
        functools.partial(kernel, planes, head_parts, heads, blocks),
        out_shape=(
            jax.ShapeDtypeStruct((rows, feat), BF16),
            jax.ShapeDtypeStruct((rows, size), F32),
        ),
        in_specs=[hbm] * 5,
        out_specs=(pl.BlockSpec(memory_space=pltpu.VMEM), pl.BlockSpec(memory_space=pltpu.VMEM)),
        scratch_shapes=[
            pltpu.VMEM((rows, feat), BF16),
            pltpu.VMEM((rows, feat), BF16),
            pltpu.VMEM((rows, feat), BF16),
            pltpu.VMEM((rows, feat), F32),
            pltpu.VMEM((max(blocks - 1, 1), heads, size, size), F32),
            pltpu.VMEM((2, blocks, BLOCK, BLOCK), BF16),
            pltpu.VMEM((2, blocks, BLOCK, BLOCK), BF16),
            states(2 * groups, F32),
            states(2 * groups, F32),
            states(groups, F32),
            *[states(2 * groups, BF16)] * 4,
            *[states(groups, BF16)] * 6,
            pltpu.VMEM((BLOCK // 2, BLOCK), F32),
            pltpu.VMEM((blocks, BLOCK, BLOCK), F32),
            pltpu.VMEM((blocks, BLOCK, size), F32),
            pltpu.VMEM((blocks, BLOCK, size), F32),
            pltpu.VMEM((rows, size), F32),
            pltpu.VMEM((8, rows), F32),
            pltpu.VMEM((head_parts, 8, rows), F32),
            pltpu.SMEM(slopes.shape, F32),
            pltpu.SMEM(doc_lengths.shape, jnp.int32),
            dma(2),
            *[dma(groups)] * 3,
            *[dma(groups)] * 2,
            *[dma(2 * groups * CUT)] * 2,
            *[dma(groups * CUT)] * 6,
            dma(head_parts),
            dma(head_parts),
        ],
        compiler_params=pltpu.CompilerParams(
            collective_id=0, has_side_effects=True, vmem_limit_bytes=47 * 1024 * 1024
        ),
    )(
        pltpu.with_memory_space_constraint(slopes, pltpu.HBM),
        pltpu.with_memory_space_constraint(doc_lengths, pltpu.HBM),
        queries, key_rows, values,
    )
    vmem = pl.BlockSpec(memory_space=pltpu.VMEM)
    return pl.pallas_call(
        scale_kernel,
        out_shape=jax.ShapeDtypeStruct((rows, feat), BF16),
        in_specs=[vmem, vmem, vmem],
        out_specs=pl.BlockSpec(memory_space=pltpu.HBM),
        scratch_shapes=[pltpu.VMEM((rows, feat), BF16), pltpu.SemaphoreType.DMA((8,))],
        compiler_params=pltpu.CompilerParams(vmem_limit_bytes=9 * 1024 * 1024),
    )(mixed, inverse, norm_gain.reshape(1, feat))


def solution(mesh):
    placed = (P("seq", "head"), P("seq", "head"), P("seq", "head"), P("head"), P(), P("head"))
    return jax.shard_map(
        functools.partial(shards, mesh.shape["seq"] // 4, mesh.shape["head"]),
        mesh=mesh, in_specs=placed, out_specs=P("seq", "head"), check_vma=False,
    )
```

```python
import functools

import jax
import jax.numpy as jnp
from jax import lax
from jax.experimental import pallas as pl
from jax.experimental.pallas import tpu as pltpu
from jax.sharding import PartitionSpec as P

BLOCK = 256
FAR = 1e30
LOG2E = 1.4426950408889634
F32 = jnp.float32
BF16 = jnp.bfloat16
MESH = pl.DeviceIdType.MESH
CUT = 1
HOPS = 14
XLAG = 4
XTRIP = 4
CTRIP = 2
LATE = 2


def kernel(
    planes, head_parts, heads, blocks,
    slopes_hbm, docs_hbm, q_hbm, k_hbm, v_hbm,
    out_ref, inv_ref,
    q_ref, k_ref, v_ref, mixed_ref, local_ref, even_ref, odd_ref, own_ref, carry_ref, chip_ref,
    s_send, s_recv, c_send, c_recv, a_send, a_recv, p_send, p_recv, x_send, x_recv,
    lag_ref, same_ref, tail_ref, lead_ref, sq_ref, sq_send, sq_recv,
    slopes_ref, docs_ref, small_sem, kv_sem,
    s_out, s_in, c_out, c_in, a_out, a_in, p_out, p_in, x_out, x_in, sq_out, sq_in,
):
    groups = heads // 4
    rows = blocks * BLOCK
    size = q_ref.shape[1] // heads
    piece = size // CUT
    late = min(LATE, groups)

    def load(hbm, ref, sem, w):
        wide = pl.ds(pl.multiple_of(w * 4 * size, 4 * size), 4 * size)
        return pltpu.make_async_copy(hbm.at[:, wide], ref.at[:, wide], sem.at[w])

    def each(count, body, start=0):
        def turn(i, _):
            body(i)
            return 0
        lax.fori_loop(start, count, turn, 0)

    def begin_kv(w):
        load(k_hbm, k_ref, kv_sem, w).start()
        load(v_hbm, v_ref, kv_sem, w).start()

    slopes_copy = pltpu.make_async_copy(slopes_hbm, slopes_ref, small_sem.at[0])
    docs_copy = pltpu.make_async_copy(docs_hbm, docs_ref, small_sem.at[1])
    begin_kv(0)
    docs_copy.start()
    slopes_copy.start()
    each(groups, begin_kv, 1)

    seq = lax.axis_index("seq")
    headpos = lax.axis_index("head")
    core = lax.rem(seq, 2)
    side = lax.rem(lax.div(seq, 2), 2)
    plane = lax.div(seq, 4)
    partner = seq + 1 - 2 * core
    across = seq + 2 - 4 * side
    ahead = jnp.minimum(seq + 4, 4 * planes - 1)

    chain_at = lax.div(HOPS * plane, 3)

    barrier = pltpu.get_barrier_semaphore()
    pl.semaphore_signal(barrier, inc=1, device_id={"seq": partner}, device_id_type=MESH)
    pl.semaphore_signal(barrier, inc=1, device_id={"seq": across}, device_id_type=MESH)

    @pl.when(plane < planes - 1)
    def _():
        pl.semaphore_signal(barrier, inc=1, device_id={"seq": seq + 4}, device_id_type=MESH)

    @pl.when(plane > 0)
    def _():
        pl.semaphore_signal(barrier, inc=1, device_id={"seq": seq - 4}, device_id_type=MESH)

    for i in range(1, head_parts):
        pl.semaphore_signal(
            barrier, inc=1, device_id={"head": lax.rem(headpos + i, head_parts)}, device_id_type=MESH
        )

    def cols(h, wide=1):
        return pl.ds(pl.multiple_of(h * size, wide * size), wide * size)

    def remote(src, dst, first, count, sem_at, out_sem, in_sem, target):
        part = pl.ds(first, count)
        return pltpu.make_async_remote_copy(
            src_ref=src.at[part], dst_ref=dst.at[part],
            send_sem=out_sem.at[0], recv_sem=in_sem.at[sem_at],
            device_id={"seq": target}, device_id_type=MESH,
        )

    def s_copy(w):
        return remote(s_send, s_recv, 2 * w * CUT, 2 * CUT, w, s_out, s_in, partner)

    def c_copy(n):
        return remote(c_send, c_recv, n, 1, lax.div(n, CUT), c_out, c_in, partner)

    def c_head(n):
        return remote(c_send, c_recv, n * CUT, CUT, n, c_out, c_in, partner)

    def a_copy(j):
        return remote(a_send, a_recv, j, 1, j, a_out, a_in, across)

    def p_copy(j):
        return remote(p_send, p_recv, j, 1, j, p_out, p_in, ahead)

    def x_copy(j):
        return remote(x_send, x_recv, j, 1, j, x_out, x_in, across)

    down = lax.broadcasted_iota(jnp.int32, (BLOCK, BLOCK), 0)
    along = lax.broadcasted_iota(jnp.int32, (BLOCK, BLOCK), 1)
    lag = jnp.where(down >= along, (down - along).astype(F32), F32(FAR))
    lag_ref[...] = lag[BLOCK // 2:]
    offs = lax.broadcasted_iota(jnp.int32, (BLOCK, size), 0)
    rem = (BLOCK - 1 - offs).astype(F32)
    reach = (offs + 1).astype(F32)
    sq_ref[...] = jnp.zeros_like(sq_ref)

    docs_copy.wait()
    slopes_copy.wait()
    starts = []
    total = jnp.int32(0)
    for j in range(docs_ref.shape[0] - 1):
        total = total + docs_ref[j]
        starts.append(total)

    def segment(pos):
        counted = jnp.zeros_like(pos)
        for s in starts:
            counted = counted + jnp.where(pos >= s, 1, 0)
        return jnp.where(pos < 0, -1, counted)

    def joined(a, b):
        return jnp.where(segment(a) == segment(b), F32(1), F32(0))

    base = seq * rows
    chip = base - core * rows
    within = []
    for b in range(blocks):
        b0 = base + b * BLOCK
        row_seg = segment(b0 + offs)
        tail_ref[b] = jnp.where(row_seg == segment(b0 + BLOCK - 1), rem, F32(FAR))
        lead_ref[b] = jnp.where(row_seg == segment(b0 - 1), reach, F32(FAR))
        within.append(joined(b0 - 1, b0 + BLOCK - 1))
    board = chip - 2 * side * rows
    j_cores = joined(chip + rows - 1, chip + 2 * rows - 1)
    j_enter = joined(chip - 1, chip + rows - 1)
    j_chips = joined(board + 2 * rows - 1, board + 4 * rows - 1)
    j_board = joined(board - 1, board + 4 * rows - 1)
    j_front = joined(board - 1, board + 2 * rows - 1)

    def rate(h):
        return slopes_ref[h] * F32(-LOG2E)

    def fade(h, distance, keep):
        return jnp.exp2(jnp.full((1, size), rate(h) * distance, F32)) * keep

    @pl.when(plane == 0)
    def _():
        p_recv[...] = jnp.zeros_like(p_recv)

    def end_state(h):
        state = None
        for b in range(blocks):
            here = pl.ds(b * BLOCK, BLOCK)
            scale = jnp.exp2(tail_ref[b] * rate(h))
            weighted = (scale * v_ref[here, cols(h)].astype(F32)).astype(BF16)
            one = lax.dot_general(
                k_ref[here, cols(h)], weighted, (((0,), (0,)), ((), ())), preferred_element_type=F32
            )
            if b < blocks - 1:
                local_ref[b, h] = one
            state = one if state is None else fade(h, F32(BLOCK), within[b]) * state + one
        return state

    def cut(i):
        return slice(i * piece, (i + 1) * piece)

    def ends(w):
        both_wide = pl.ds(0, 8 * size)
        pltpu.make_async_copy(k_hbm.at[:, both_wide], k_ref.at[:, both_wide], kv_sem.at[w]).wait()
        load(q_hbm, q_ref, kv_sem, w).start()
        for b0 in range(2):
            state = end_state(4 * w + 2 * (1 - core) + b0).astype(BF16)
            for i in range(CUT):
                s_send[(2 * w + b0) * CUT + i] = state[cut(i)]
        for b0 in range(2):
            state = end_state(4 * w + 2 * core + b0)
            for i in range(CUT):
                own_ref[(2 * w + b0) * CUT + i] = state[cut(i)]

    is_second = core == 1
    is_after = side == 1

    def core_states(n):
        here, there = own_ref[n], s_recv[n].astype(F32)
        return jnp.where(is_second, there, here), jnp.where(is_second, here, there)

    def chip_state(h, n):
        early, late_one = core_states(n)
        return fade(h, F32(rows), j_cores) * early + late_one

    def give_head(w):
        return 4 * w + 2 * core + (1 - side)

    def keep_head(w):
        return 4 * w + 2 * core + side

    def give(w):
        s_copy(w).wait_recv()
        for i in range(CUT):
            n = (2 * w + (1 - side)) * CUT + i
            a_send[w * CUT + i] = chip_state(give_head(w), n).astype(BF16)
        for i in range(CUT):
            a_copy(w * CUT + i).start()
        for i in range(CUT):
            n = (2 * w + side) * CUT + i
            chip_ref[w * CUT + i] = chip_state(keep_head(w), n)

    def settle(h, n, enters):
        early, _ = core_states(n)
        second = fade(h, F32(rows), j_enter) * enters + early
        carry_ref[n] = jnp.where(is_second, second, enters)
        c_send[n] = jnp.where(is_second, enters, second).astype(BF16)
        c_copy(n).start()

    def chain(w):
        h = keep_head(w)
        for i in range(CUT):
            j = w * CUT + i
            a_copy(j).wait_recv()

            @pl.when(plane > 0)
            def _():
                p_copy(j).wait_recv()

            here, there = chip_ref[j], a_recv[j].astype(F32)
            early, late_one = jnp.where(is_after, there, here), jnp.where(is_after, here, there)
            before = p_recv[j].astype(F32)
            total = fade(h, F32(2 * rows), j_chips) * early + late_one
            p_send[j] = (fade(h, F32(4 * rows), j_board) * before + total).astype(BF16)

            @pl.when(plane < planes - 1)
            def _():
                p_copy(j).start()

            second = fade(h, F32(2 * rows), j_front) * before + early
            x_send[j] = jnp.where(is_after, before, second).astype(BF16)

            @pl.when(chain_at >= XLAG)
            def _():
                x_copy(j).start()

            settle(h, (2 * w + side) * CUT + i, jnp.where(is_after, second, before))

    def x_start(w):
        for i in range(CUT):
            x_copy(w * CUT + i).start()

    def over(w):
        for i in range(CUT):
            j = w * CUT + i
            x_copy(j).wait_recv()
            settle(give_head(w), (2 * w + (1 - side)) * CUT + i, x_recv[j].astype(F32))

    mid = BLOCK // 2
    for ref in (even_ref, odd_ref):
        for i in range(2):
            for b in range(blocks):
                ref[i, b, :mid, mid:] = jnp.zeros((mid, BLOCK - mid), BF16)

    for b in range(blocks):
        b0 = base + b * BLOCK
        same_ref[b] = jnp.where(segment(b0 + down) == segment(b0 + along), F32(1), F32(0))

    def weigh_one(u, ref, i, b, decay):
        h = 2 * u + i
        here = pl.ds(b * BLOCK, BLOCK)
        scores = lax.dot_general(
            q_ref[here, cols(h)], k_ref[here, cols(h)], (((1,), (1,)), ((), ())),
            preferred_element_type=F32,
        )
        ref[i, b, :mid, :mid] = (
            scores[:mid, :mid] * decay[:, mid:] * same_ref[b, :mid, :mid]
        ).astype(BF16)
        ref[i, b, mid:, :] = (scores[mid:] * decay * same_ref[b, mid:, :]).astype(BF16)

    def apply_one(u, ref, i, b):
        h = 2 * u + i
        here = pl.ds(b * BLOCK, BLOCK)
        mixed_ref[here, cols(h)] = jnp.dot(
            ref[i, b], v_ref[here, cols(h)], preferred_element_type=F32
        )

    def weigh(u, ref):
        for i in range(2):
            decay = jnp.exp2(lag_ref[...] * rate(2 * u + i))
            for b in range(blocks):
                weigh_one(u, ref, i, b, decay)

    def apply(u, ref):
        for i in range(2):
            for b in range(blocks):
                apply_one(u, ref, i, b)

    units = heads // 2

    def both(f, fref, u, uref):
        apply(u, uref)
        weigh(f, fref)

    def intra(u):
        following = jnp.minimum(u + 1, units - 1)

        @pl.when(lax.rem(u, 2) == 0)
        def _():
            both(following, odd_ref, u, even_ref)

        @pl.when((lax.rem(u, 2) == 1) & (u < units - 1))
        def _():
            load(q_hbm, q_ref, kv_sem, lax.div(following, 2)).wait()

        @pl.when(lax.rem(u, 2) == 1)
        def _():
            both(following, even_ref, u, odd_ref)

    def finish(pair, states):
        blank = jnp.zeros((size, size), BF16)
        for b in range(blocks):
            first, second = states[0].astype(BF16), states[1].astype(BF16)
            joint = jnp.concatenate(
                [jnp.concatenate([first, blank], axis=1), jnp.concatenate([blank, second], axis=1)],
                axis=0,
            )
            for r in range(0, BLOCK, BLOCK // 2):
                here = pl.ds(b * BLOCK + r, BLOCK // 2)
                both_q = jnp.concatenate([q_ref[here, cols(h)] for h in pair], axis=1)
                inter = jnp.dot(both_q, joint, preferred_element_type=F32)
                squares = sq_ref[here, :]
                lead = lead_ref[b, r:r + BLOCK // 2]
                for i in range(2):
                    scale = jnp.exp2(lead * rate(pair[i]))
                    mixed = mixed_ref[here, cols(pair[i])] + inter[:, i * size:(i + 1) * size] * scale
                    squares = squares + mixed * mixed
                    out_ref[here, cols(pair[i])] = mixed.astype(BF16)
                sq_ref[here, :] = squares
            if b < blocks - 1:
                states = [
                    fade(pair[i], F32(BLOCK), within[b]) * states[i] + local_ref[b, pair[i]]
                    for i in range(2)
                ]

    def whole(ref, w, b0):
        parts = [ref[(2 * w + b0) * CUT + i] for i in range(CUT)]
        return parts[0] if CUT == 1 else jnp.concatenate(parts, axis=0)

    def finish_pair(w, b0):
        c_head(2 * w + b0).wait_recv()
        finish(
            (4 * w + 2 * core + b0, 4 * w + 2 * (1 - core) + b0),
            [whole(carry_ref, w, b0), whole(c_recv, w, b0).astype(F32)],
        )

    def kept(w):
        finish_pair(w, side)

    def given(w):
        finish_pair(w, 1 - side)

    def ends_step(w):
        ends(w)

        @pl.when(w == 0)
        def _():
            beside = jnp.where(plane > 0, 1, 0) + jnp.where(plane < planes - 1, 1, 0)
            pl.semaphore_wait(barrier, 1 + head_parts + beside)

        s_copy(w).start()

        @pl.when(w >= late)
        def _():
            give(w - late)

    each(groups, ends_step)
    x_at = jnp.maximum(chain_at, XLAG)
    over_at = jnp.minimum(x_at + XTRIP + 2, jnp.maximum(x_at + XTRIP, units - 2))
    kept_at = jnp.maximum(chain_at + CTRIP, units)
    given_at = jnp.maximum(over_at + CTRIP, units + 1)
    last_x = max(HOPS * (planes - 1) // 3, XLAG)
    last_over = min(last_x + XTRIP + 2, max(last_x + XTRIP, units - 2))
    slots = max(last_over + CTRIP, units + 1) + groups

    def when_in(t, start, count, body):
        @pl.when((t >= start) & (t < start + count))
        def _():
            body(t - start)

    def hand_on(t):
        when_in(t, 0, late, lambda n: give(groups - late + n))
        when_in(t, chain_at, groups, chain)

    def slot(t):
        hand_on(t)

        @pl.when(chain_at < XLAG)
        def _():
            when_in(t, x_at, groups, x_start)

        when_in(t, over_at, groups, over)
        when_in(t, 0, units, intra)

        when_in(t, kept_at, groups, kept)
        when_in(t, given_at, groups, given)

    load(q_hbm, q_ref, kv_sem, 0).wait()
    weigh(jnp.int32(0), even_ref)
    each(slots, slot)

    ones = jnp.ones((8, size), F32)
    summed = lax.dot_general(
        ones, sq_ref[...], (((1,), (1,)), ((), ())),
        precision=lax.Precision.HIGHEST, preferred_element_type=F32,
    )
    sq_send[...] = summed

    def sq_copy(i):
        return pltpu.make_async_remote_copy(
            src_ref=sq_send, dst_ref=sq_recv.at[i - 1],
            send_sem=sq_out.at[i - 1], recv_sem=sq_in.at[i - 1],
            device_id={"head": lax.rem(headpos + i, head_parts)}, device_id_type=MESH,
        )

    for i in range(1, head_parts):
        sq_copy(i).start()

    count = groups * CUT
    remote(s_send, s_recv, 0, 2 * count, 0, s_out, s_in, partner).wait_send()
    remote(c_send, c_recv, 0, 2 * count, 0, c_out, c_in, partner).wait_send()
    remote(a_send, a_recv, 0, count, 0, a_out, a_in, across).wait_send()
    remote(x_send, x_recv, 0, count, 0, x_out, x_in, across).wait_send()

    @pl.when(plane < planes - 1)
    def _():
        remote(p_send, p_recv, 0, count, 0, p_out, p_in, ahead).wait_send()

    for i in range(1, head_parts):
        sq_copy(i).wait_recv()
        summed = summed + sq_recv[i - 1]
    inverse = lax.rsqrt(summed / F32(heads * size * head_parts) + F32(1e-05))
    inv_ref[...] = jnp.broadcast_to(jnp.transpose(inverse)[:, 0:1], inv_ref.shape)
    for i in range(1, head_parts):
        sq_copy(i).wait_send()


def scale_kernel(mixed_ref, inv_ref, gain_ref, final_hbm, final_ref, sem):
    rows, size = inv_ref.shape
    strip = rows // sem.shape[0]

    def move(i):
        here = pl.ds(i * strip, strip)
        return pltpu.make_async_copy(final_ref.at[here], final_hbm.at[here], sem.at[i])

    for i in range(sem.shape[0]):
        here = pl.ds(i * strip, strip)
        inverse = inv_ref[here, :]
        for c in range(0, final_ref.shape[1], size):
            piece = mixed_ref[here, c:c + size].astype(F32)
            final_ref[here, c:c + size] = (piece * inverse * gain_ref[:, c:c + size]).astype(BF16)
        move(i).start()
    for i in range(sem.shape[0]):
        move(i).wait()


def shards(planes, head_parts, queries, key_rows, values, slopes, doc_lengths, norm_gain):
    rows, feat = queries.shape
    heads = slopes.shape[0]
    size = feat // heads
    blocks = rows // BLOCK
    groups = heads // 4
    hbm = pl.BlockSpec(memory_space=pltpu.HBM)
    piece = size // CUT
    states = lambda count, dtype: pltpu.VMEM((count * CUT, piece, size), dtype)
    dma = lambda n: pltpu.SemaphoreType.DMA((n,))
    mixed, inverse = pl.pallas_call(
        functools.partial(kernel, planes, head_parts, heads, blocks),
        out_shape=(
            jax.ShapeDtypeStruct((rows, feat), BF16),
            jax.ShapeDtypeStruct((rows, size), F32),
        ),
        in_specs=[hbm] * 5,
        out_specs=(pl.BlockSpec(memory_space=pltpu.VMEM), pl.BlockSpec(memory_space=pltpu.VMEM)),
        scratch_shapes=[
            pltpu.VMEM((rows, feat), BF16),
            pltpu.VMEM((rows, feat), BF16),
            pltpu.VMEM((rows, feat), BF16),
            pltpu.VMEM((rows, feat), F32),
            pltpu.VMEM((max(blocks - 1, 1), heads, size, size), F32),
            pltpu.VMEM((2, blocks, BLOCK, BLOCK), BF16),
            pltpu.VMEM((2, blocks, BLOCK, BLOCK), BF16),
            states(2 * groups, F32),
            states(2 * groups, F32),
            states(groups, F32),
            *[states(2 * groups, BF16)] * 4,
            *[states(groups, BF16)] * 6,
            pltpu.VMEM((BLOCK // 2, BLOCK), F32),
            pltpu.VMEM((blocks, BLOCK, BLOCK), F32),
            pltpu.VMEM((blocks, BLOCK, size), F32),
            pltpu.VMEM((blocks, BLOCK, size), F32),
            pltpu.VMEM((rows, size), F32),
            pltpu.VMEM((8, rows), F32),
            pltpu.VMEM((max(head_parts - 1, 1), 8, rows), F32),
            pltpu.SMEM(slopes.shape, F32),
            pltpu.SMEM(doc_lengths.shape, jnp.int32),
            dma(2),
            dma(groups),
            dma(1), dma(groups),
            dma(1), dma(2 * groups),
            *[dma(1), dma(groups * CUT)] * 3,
            *[dma(max(head_parts - 1, 1))] * 2,
        ],
        compiler_params=pltpu.CompilerParams(
            collective_id=0, has_side_effects=True, vmem_limit_bytes=47 * 1024 * 1024
        ),
    )(
        pltpu.with_memory_space_constraint(slopes, pltpu.HBM),
        pltpu.with_memory_space_constraint(doc_lengths, pltpu.HBM),
        queries, key_rows, values,
    )
    vmem = pl.BlockSpec(memory_space=pltpu.VMEM)
    return pl.pallas_call(
        scale_kernel,
        out_shape=jax.ShapeDtypeStruct((rows, feat), BF16),
        in_specs=[vmem, vmem, vmem],
        out_specs=pl.BlockSpec(memory_space=pltpu.HBM),
        scratch_shapes=[pltpu.VMEM((rows, feat), BF16), pltpu.SemaphoreType.DMA((8,))],
        compiler_params=pltpu.CompilerParams(vmem_limit_bytes=9 * 1024 * 1024),
    )(mixed, inverse, norm_gain.reshape(1, feat))


def solution(mesh):
    placed = (P("seq", "head"), P("seq", "head"), P("seq", "head"), P("head"), P(), P("head"))
    return jax.shard_map(
        functools.partial(shards, mesh.shape["seq"] // 4, mesh.shape["head"]),
        mesh=mesh, in_specs=placed, out_specs=P("seq", "head"), check_vma=False,
    )
```
